32 devices in a mesh: segment: 2 (over x), rows: 8 (over z, y), cols: 2 (over core).
Axes of the slice: x: 2, y: 2, z: 4, core: 2. Of those that a mesh axis runs over, the one named last changes fastest.
Arguments:
- frames: bfloat16 [2, 2, 16, 128, 128], P(None, None, 'rows', 'cols'), may hold values from -6 to 6
- cell_weight: bfloat16 [9, 256, 512], P(None, 'rows'), may hold values from -0.125 to 0.125
- cell_bias: float32 [512], replicated, may hold values from -3 to 3
- first_context_weight: bfloat16 [9, 128, 384], P(None, 'rows'), may hold values from -1 to 1
- first_context_bias: float32 [384], replicated, may hold values from -0.5 to 1
- second_context_weight: bfloat16 [9, 384, 384], P(None, 'rows'), may hold values from -0.109375 to 0.109375
- second_context_bias: float32 [384], replicated, may hold values from -0.5 to 1
- third_context_weight: bfloat16 [9, 384, 384], P(None, 'rows'), may hold values from -0.109375 to 0.109375
- third_context_bias: float32 [384], replicated, may hold values from 0 to 1
Outputs:
- context: bfloat16 [2, 16, 128, 384], P('segment', 'rows', 'cols')
The draws below stay inside these ranges and needn't reach their ends.
All inputs are finite; a program needn't handle non-finite values.
Results may differ from the reference program's by a relative error of at most 0.0065.
Values may be sent and summed in bfloat16 or wider, within the bound.
A program may use at most 64 MiB of HBM per device.

```python
import jax
import jax.numpy as jnp
from jax import lax

C = 128
CIN = 128
K = 384
STEPS = 2
MB = 2
FIRST_DILATION = 16
SECOND_DILATION = 32
THIRD_DILATION = 64
NH = 16
NW = 128


def shard_levels(own_key, dims, shards, smallest, largest):
    level, own = 1.0, jax.random.fold_in(own_key, 6)
    for dim, parts in shards:
        heights = jnp.exp(jax.random.uniform(jax.random.fold_in(own, dim), (parts,), jnp.float32, smallest / len(shards), largest / len(shards)))
        level = level * jnp.repeat(heights, dims[dim] // parts).reshape([-1 if axis == dim else 1 for axis in range(len(dims))])
    return level


def centred(stream_key, shape, width, reach, pieces=(), dtype=jnp.bfloat16):
    level = shard_levels(stream_key, shape, pieces, -0.22, 0.18) if pieces else 1.0
    values = jax.random.normal(stream_key, shape, jnp.float32) * width * level
    return jnp.minimum(jnp.maximum(values, -reach), reach).astype(dtype)


def setup_inputs(seed: int = 0) -> dict:
    streams_of = jax.random.split(jax.random.key(seed), 10)
    frames = centred(streams_of[0], (MB, STEPS, NH, NW, CIN), 1.0, 6.0, ((2, 8), (3, 2)))
    cell_weight = centred(streams_of[1], (9, CIN + C, 4 * C), (9 * (CIN + C)) ** -0.5, 0.125, ((1, 8),))
    cell_bias = centred(streams_of[2], (4 * C,), 0.5, 3.0, (), jnp.float32)
    first_context_weight = centred(streams_of[3], (9, C, K), (C // 4) ** -0.5, 1.0, ((1, 8),))
    first_context_bias = jnp.clip(jax.random.uniform(streams_of[4], (K,), jnp.float32, -0.5, 1.0), -0.5, 1.0)
    second_context_weight = centred(streams_of[5], (9, K, K), (9 * K) ** -0.5, 0.109375, ((1, 8),))
    second_context_bias = jnp.clip(jax.random.uniform(streams_of[6], (K,), jnp.float32, -0.5, 1.0), -0.5, 1.0)
    third_context_weight = centred(streams_of[7], (9, K, K), (9 * K) ** -0.5, 0.109375, ((1, 8),))
    third_context_bias = jnp.clip(jax.random.uniform(streams_of[8], (K,), jnp.float32, 0.0, 1.0), 0.0, 1.0)
    return dict(frames=frames, cell_weight=cell_weight, cell_bias=cell_bias, first_context_weight=first_context_weight, first_context_bias=first_context_bias, second_context_weight=second_context_weight, second_context_bias=second_context_bias, third_context_weight=third_context_weight, third_context_bias=third_context_bias)


def dilated_convolve(feature, weight, spacing):
    kernel = weight.astype(jnp.float32).reshape(3, 3, weight.shape[1], weight.shape[2])
    result = lax.conv_general_dilated(
        feature.astype(jnp.float32)[None], kernel, (1, 1),
        [(spacing, spacing), (spacing, spacing)], rhs_dilation=(spacing, spacing),
        dimension_numbers=("NHWC", "HWIO", "NHWC"), precision=lax.Precision.HIGHEST)
    return result[0]


def reference(frames, cell_weight, cell_bias, first_context_weight, first_context_bias, second_context_weight, second_context_bias, third_context_weight, third_context_bias):
    outputs = []
    for micro_index in range(MB):
        hidden_state = jnp.zeros((NH, NW, C), jnp.bfloat16)
        memory = jnp.zeros((NH, NW, C), jnp.float32)
        for moment in range(STEPS):
            joined = jnp.concatenate([frames[micro_index, moment], hidden_state], axis=-1)
            gate_sums = dilated_convolve(joined, cell_weight, 1) + cell_bias
            inflow = jax.nn.sigmoid(gate_sums[..., :C])
            forget = jax.nn.sigmoid(gate_sums[..., C:2 * C])
            output = jax.nn.sigmoid(gate_sums[..., 2 * C:3 * C])
            update = jnp.tanh(gate_sums[..., 3 * C:])
            memory = forget * memory + inflow * update
            hidden_state = (output * jnp.tanh(memory)).astype(jnp.bfloat16)
        first_output = jnp.maximum(dilated_convolve(hidden_state, first_context_weight, FIRST_DILATION) + first_context_bias, 0.0).astype(jnp.bfloat16)
        second_output = jnp.maximum(dilated_convolve(first_output, second_context_weight, SECOND_DILATION) + second_context_bias, 0.0).astype(jnp.bfloat16)
        third_output = jnp.maximum(dilated_convolve(second_output, third_context_weight, THIRD_DILATION) + third_context_bias, 0.0)
        outputs.append((second_output.astype(jnp.float32) + third_output).astype(jnp.bfloat16))
    return jnp.stack(outputs)
```

```python
import jax
import jax.numpy as jnp
from jax import lax
from jax.experimental import pallas as pl
from jax.experimental.pallas import tpu as pltpu
from jax.sharding import PartitionSpec as P

DILATIONS = (16, 32, 64)
MESH_ID = pl.DeviceIdType.MESH
MARGIN = 16


def encoder_kernel(
    frames, cell_w, cell_b, first_w, first_b, second_w, second_b, third_w, third_b,
    out, wc, w1, w2, w3, fp, hp, f1, f2, f3,
    local_sem, ring_s, ring_r, pair_s, pair_r, ex_s, ex_r, *, n, cols, row_pads,
):
    seg, r, c = lax.axis_index("segment"), lax.axis_index("rows"), lax.axis_index("cols")
    steps, height, across, channels = frames.shape[1:]
    state = cell_b.shape[-1] // 4
    half = n // 2
    odd = c % 2
    even_core, odd_core = odd == 0, odd == 1
    sign = 1 - 2 * odd
    parity = r % 2
    place = (1 - parity) * (r // 2) + parity * (n - 1 - r // 2)

    def rows_at(position):
        upper = position // half
        return (1 - upper) * 2 * position + upper * (2 * (n - 1 - position) + 1)

    following = rows_at((place + sign + n) % n)
    preceding = rows_at((place - sign + n) % n)
    partner = c + 1 - 2 * odd
    ahead_id, partner_id = (seg, following, c), (seg, r, partner)

    reaches = sorted({1} | {s // height for s, pad in zip(DILATIONS, row_pads) if pad})
    offsets = [(0, -1), (0, 1)] + [
        (d * reach, dc) for reach in reaches for d in (-1, 1) for dc in (-1, 0, 1)
    ]

    def present(dr, dc):
        row, col = r + dr, c + dc
        return jnp.logical_and(
            jnp.logical_and(row >= 0, row < n), jnp.logical_and(col >= 0, col < cols)
        )

    locals_ = []
    for t in range(steps):
        locals_.append(
            pltpu.make_async_copy(
                frames.at[seg, t],
                fp.at[t, pl.ds(1, height), pl.ds(MARGIN, across)],
                local_sem.at[t],
            )
        )
    stored = (cell_w, first_w, second_w, third_w)
    gathered = (wc, w1, w2, w3)
    own = []
    for ref, whole in zip(stored, gathered):
        taps = whole.shape[1]
        own.append(ref.at[pl.ds((9 - taps) // 2, taps)])
    for a in range(4):
        locals_.append(
            pltpu.make_async_copy(own[a], gathered[a].at[r], local_sem.at[steps + a])
        )
    for t in range(steps):
        fp[t] = jnp.zeros(fp.shape[1:], fp.dtype)
    for t in range(hp.shape[0]):
        hp[t] = jnp.zeros(hp.shape[1:], hp.dtype)
    for buffer in (f1, f2, f3):
        buffer[...] = jnp.zeros(buffer.shape, buffer.dtype)
    for copy in locals_:
        copy.start()

    barrier = pltpu.get_barrier_semaphore()
    expected = jnp.int32(2)
    for target in (following, preceding):
        pl.semaphore_signal(barrier, inc=1, device_id=(seg, target, c), device_id_type=MESH_ID)
    for dr, dc in offsets:
        there = present(dr, dc)
        expected = expected + there.astype(jnp.int32)

        @pl.when(there)
        def _():
            pl.semaphore_signal(
                barrier, inc=1, device_id=(seg, r + dr, c + dc), device_id_type=MESH_ID
            )

    pl.semaphore_wait(barrier, expected)

    def exchange(number, source_of, buffer, pad, reach, width):
        arrivals, departures = [], []
        for i, (dr, dc) in enumerate((a, b) for a in (-1, 0, 1) for b in (-1, 0, 1)):
            if (dr, dc) == (0, 0) or (dr and not pad):
                continue
            first, span, landing = {
                -1: (0, pad, pad + height), 0: (0, height, pad), 1: (height - pad, pad, 0)
            }[dr]
            left, extent, side = {
                -1: (0, width[1], width[0] + across),
                0: (0, across, width[0]),
                1: (across - width[1], width[1], width[0] - width[1]),
            }[dc]
            copy = pltpu.make_async_remote_copy(
                src_ref=source_of(first, span, left, extent),
                dst_ref=buffer.at[pl.ds(landing, span), pl.ds(side, extent)],
                send_sem=ex_s.at[number, i],
                recv_sem=ex_r.at[number, i],
                device_id=(seg, r + dr * reach, c + dc),
                device_id_type=MESH_ID,
            )
            there, behind = present(dr * reach, dc), present(-dr * reach, -dc)
            pl.when(there)(copy.start)
            departures.append((there, copy))
            arrivals.append((behind, copy))

        def arrive():
            for behind, copy in arrivals:
                pl.when(behind)(copy.wait_recv)

        def depart():
            for there, copy in departures:
                pl.when(there)(copy.wait_send)

        return arrive, depart

    def block_of(buffer, pad, margin):
        return lambda first, span, left, extent: buffer.at[
            pl.ds(pad + first, span), pl.ds(margin + left, extent)
        ]

    departs = []
    frame_arrivals = []
    for t in range(steps):
        arrive, depart = exchange(
            t,
            lambda first, span, left, extent, t=t: frames.at[
                seg, t, pl.ds(first, span), pl.ds(left, extent)
            ],
            fp.at[t], 1, 1, (MARGIN, MARGIN),
        )
        frame_arrivals.append(arrive)
        departs.append(depart)

    def ring_copy(a, k):
        slot = gathered[a].at[rows_at((place - sign * k + n) % n)]
        return pltpu.make_async_remote_copy(
            src_ref=own[a] if k == 0 else slot,
            dst_ref=slot,
            send_sem=ring_s.at[a, k],
            recv_sem=ring_r.at[a, k],
            device_id=ahead_id,
            device_id_type=MESH_ID,
        )

    def arriving(a, k):
        slot = gathered[a].at[rows_at((place - sign * k + n) % n)]
        return pltpu.make_async_remote_copy(
            src_ref=slot, dst_ref=slot, send_sem=ring_s.at[a, k - 1],
            recv_sem=ring_r.at[a, k - 1], device_id=ahead_id, device_id_type=MESH_ID,
        )

    def pair_copy(a, k, direction):
        slot = gathered[a].at[rows_at((place - direction * sign * k + n) % n)]
        return pltpu.make_async_remote_copy(
            src_ref=slot, dst_ref=slot, send_sem=pair_s.at[a, k], recv_sem=pair_r.at[a, k],
            device_id=partner_id, device_id_type=MESH_ID,
        )

    def longer(a):
        return even_core if a == 0 else odd_core

    def guarded(condition, act):
        if condition is None:
            act()
        else:
            pl.when(condition)(act)

    def ring_send(a, k):
        guarded(longer(a) if k == half - 1 else None, ring_copy(a, k).start)

    def ring_step(a, k):
        def act():
            arriving(a, k).wait_recv()
            if k < half:
                ring_send(a, k)
            pair_copy(a, k, 1).start()

        guarded(longer(a) if k == half else None, act)

    def pair_waits(a):
        for k in range(1, half + 1):
            shorter = odd_core if a == 0 else even_core
            guarded(shorter if k == half else None, pair_copy(a, k, -1).wait_recv)

    ring_send(0, 0)
    for k in range(1, half + 1):
        ring_step(0, k)
        if k <= 3:
            ring_send(k, 0)
    for k in range(half + 1, 4):
        ring_send(k, 0)

    for copy in locals_:
        copy.wait()
    for arrive in frame_arrivals:
        arrive()
    pair_waits(0)

    bias = cell_b[...]
    per = wc.shape[2]
    frame_sources = channels // per

    def tap_columns(buffer):
        taps = []
        for row in range(height + 2):
            wide = buffer[row].astype(jnp.float32)
            length = wide.shape[0]
            taps.append(
                [
                    pltpu.roll(wide, 1, 0)[MARGIN : MARGIN + across].astype(jnp.bfloat16),
                    buffer[row, MARGIN : MARGIN + across],
                    pltpu.roll(wide, length - 1, 0)[MARGIN : MARGIN + across].astype(
                        jnp.bfloat16
                    ),
                ]
            )
        return taps

    def gate_part(buffer, sources):
        taps = tap_columns(buffer)
        left = jnp.concatenate(
            [
                jnp.concatenate([taps[row + a][b] for row in range(height)], axis=0)
                for a in range(3)
                for b in range(3)
            ],
            axis=1,
        )
        right = jnp.concatenate([wc[s, t] for t in range(9) for s in sources], axis=0)
        return jnp.dot(left, right, preferred_element_type=jnp.float32)

    def update(gates, memory):
        inflow = jax.nn.sigmoid(gates[:, :state])
        forget = jax.nn.sigmoid(gates[:, state : 2 * state])
        output = jax.nn.sigmoid(gates[:, 2 * state : 3 * state])
        fresh = inflow * jnp.tanh(gates[:, 3 * state :])
        memory = fresh if memory is None else forget * memory + fresh
        return (output * jnp.tanh(memory)).astype(jnp.bfloat16), memory

    context_steps = list(range(1, half + 1))
    quarter = max(1, half // 4)

    def context_ring(count):
        for _ in range(min(count, len(context_steps))):
            k = context_steps.pop(0)
            for a in (1, 2, 3):
                ring_step(a, k)

    seen, unseen = range(frame_sources), range(frame_sources, n)
    hidden, memory = update(gate_part(fp.at[0], seen) + bias, None)
    for t in range(1, steps):
        view = hp.at[t - 1]
        for row in range(height):
            view[1 + row, MARGIN : MARGIN + across] = hidden[row * across : (row + 1) * across]
        arrive, depart = exchange(
            steps + t - 1, block_of(view, 1, MARGIN), view, 1, 1, (MARGIN, MARGIN)
        )
        departs.append(depart)
        context_ring(quarter)
        gates = gate_part(fp.at[t], seen) + bias
        context_ring(quarter)
        arrive()
        hidden, memory = update(gates + gate_part(view, unseen), memory)

    feature = hidden
    layers = ((f1, w1, first_b), (f2, w2, second_b), (f3, w3, third_b))
    for i, (buffer, weight, offset) in enumerate(layers):
        spacing, pad = DILATIONS[i], row_pads[i]
        for row in range(height):
            buffer[pad + row, spacing : spacing + across] = feature[
                row * across : (row + 1) * across
            ]
        arrive, depart = exchange(
            2 * steps - 1 + i, block_of(buffer, pad, spacing), buffer, pad,
            spacing // height, (spacing, spacing),
        )
        departs.append(depart)
        if i == 0:
            context_ring(len(context_steps))
        pair_waits(i + 1)
        arrive()
        total = None
        taps = weight.shape[1]
        for t in range(taps):
            a, b = t // 3, t % 3
            left = buffer[a * pad : a * pad + height, b * spacing : b * spacing + across]
            left = left.reshape(height * across, left.shape[-1])
            right = jnp.concatenate([weight[s, t] for s in range(n)], axis=0)
            product = jnp.dot(left, right, preferred_element_type=jnp.float32)
            total = product if total is None else total + product
        result = jnp.maximum(total + offset[...], 0.0)
        if i < 2:
            feature = result.astype(jnp.bfloat16)
    context = (feature.astype(jnp.float32) + result).astype(jnp.bfloat16)
    out[0] = context.reshape(out.shape[1:])

    for depart in departs:
        depart()
    for a in range(4):
        for k in range(half):
            guarded(longer(a) if k == half - 1 else None, ring_copy(a, k).wait_send)
        for k in range(1, half + 1):
            guarded(longer(a) if k == half else None, pair_copy(a, k, 1).wait_send)


def per_device(n, cols, *args):
    import functools

    frames, cell_w, cell_b, first_w, first_b, second_w, second_b, third_w, third_b = args
    micro, steps, height, across, channels = frames.shape
    state, width = cell_b.shape[0] // 4, first_b.shape[0]
    row_pads = tuple(height if s // height < n else 0 for s in DILATIONS)

    def slots(weight, pad):
        return pltpu.VMEM((n, 9 if pad else 3) + weight.shape[1:], weight.dtype)

    def field(spacing, pad, depth):
        return pltpu.VMEM((height + 2 * pad, across + 2 * spacing, depth), jnp.bfloat16)

    half = n // 2
    exchanges = 2 * steps - 1 + 3
    dma = pltpu.SemaphoreType.DMA
    anywhere, vmem = pl.BlockSpec(memory_space=pl.ANY), pl.BlockSpec(memory_space=pltpu.VMEM)
    return pl.pallas_call(
        functools.partial(encoder_kernel, n=n, cols=cols, row_pads=row_pads),
        out_shape=jax.ShapeDtypeStruct((1, height, across, width), jnp.bfloat16),
        in_specs=[anywhere, anywhere, vmem, anywhere, vmem, anywhere, vmem, anywhere, vmem],
        out_specs=vmem,
        scratch_shapes=[
            slots(cell_w, 1),
            slots(first_w, row_pads[0]),
            slots(second_w, row_pads[1]),
            slots(third_w, row_pads[2]),
            pltpu.VMEM((steps, height + 2, across + 2 * MARGIN, channels), jnp.bfloat16),
            pltpu.VMEM((steps - 1, height + 2, across + 2 * MARGIN, state), jnp.bfloat16),
            field(DILATIONS[0], row_pads[0], state),
            field(DILATIONS[1], row_pads[1], width),
            field(DILATIONS[2], row_pads[2], width),
            dma((steps + 4,)),
            dma((4, half)),
            dma((4, half)),
            dma((4, half + 1)),
            dma((4, half + 1)),
            dma((exchanges, 9)),
            dma((exchanges, 9)),
        ],
        compiler_params=pltpu.CompilerParams(collective_id=0, has_side_effects=True),
    )(
        frames, cell_w, cell_b[None], first_w, first_b[None], second_w, second_b[None],
        third_w, third_b[None],
    )


def solution(mesh):
    import functools

    kernels = P(None, "rows", None)
    placed = (
        P(None, None, "rows", "cols", None),
        kernels, P(), kernels, P(), kernels, P(), kernels, P(),
    )
    return jax.shard_map(
        functools.partial(per_device, mesh.shape["rows"], mesh.shape["cols"]),
        mesh=mesh,
        in_specs=placed,
        out_specs=P("segment", "rows", "cols", None),
        check_vma=False,
    )
```

```python
import jax
import jax.numpy as jnp
from jax import lax
from jax.experimental import pallas as pl
from jax.experimental.pallas import tpu as pltpu
from jax.sharding import PartitionSpec as P

DILATIONS = (16, 32, 64)
MESH_ID = pl.DeviceIdType.MESH
MARGIN = 16


def encoder_kernel(
    frames, cell_w, cell_b, first_w, first_b, second_w, second_b, third_w, third_b,
    out, wc, w1, w2, w3, fp, hp, f1, f2, f3,
    local_sem, ring_s, ring_r, across_s, across_r, pair_s, pair_r, ex_s, ex_r, *, n, cols, shared, row_pads,
):
    seg, r, c = lax.axis_index("segment"), lax.axis_index("rows"), lax.axis_index("cols")
    steps, height, across, channels = frames.shape[1:]
    state = cell_b.shape[-1] // 4
    half = n // 2
    odd = c % 2
    even_core, odd_core = odd == 0, odd == 1
    sign = 1 - 2 * odd
    parity = r % 2
    place = (1 - parity) * (r // 2) + parity * (n - 1 - r // 2)

    def rows_at(position):
        upper = position // half
        return (1 - upper) * 2 * position + upper * (2 * (n - 1 - position) + 1)

    following = rows_at((place + sign + n) % n)
    preceding = rows_at((place - sign + n) % n)
    partner = c + 1 - 2 * odd
    ahead_id, partner_id = (seg, following, c), (seg, r, partner)

    reaches = sorted({1} | {s // height for s, pad in zip(DILATIONS, row_pads) if pad})
    offsets = [(0, -1), (0, 1)] + [
        (d * reach, dc) for reach in reaches for d in (-1, 1) for dc in (-1, 0, 1)
    ]

    def present(dr, dc):
        row, col = r + dr, c + dc
        return jnp.logical_and(
            jnp.logical_and(row >= 0, row < n), jnp.logical_and(col >= 0, col < cols)
        )

    locals_ = []
    for t in range(steps):
        locals_.append(
            pltpu.make_async_copy(
                frames.at[seg, t],
                fp.at[t, pl.ds(1, height), pl.ds(MARGIN, across)],
                local_sem.at[t],
            )
        )
    stored = (cell_w, first_w, second_w, third_w)
    gathered = (wc, w1, w2, w3)
    own = []
    for ref, whole in zip(stored, gathered):
        taps = whole.shape[1]
        own.append(ref.at[pl.ds((9 - taps) // 2, taps)])
    for a in range(4):
        locals_.append(
            pltpu.make_async_copy(own[a], gathered[a].at[r], local_sem.at[steps + a])
        )
    for t in range(steps):
        fp[t] = jnp.zeros(fp.shape[1:], fp.dtype)
    for t in range(hp.shape[0]):
        hp[t] = jnp.zeros(hp.shape[1:], hp.dtype)
    for buffer in (f1, f2, f3):
        buffer[...] = jnp.zeros(buffer.shape, buffer.dtype)
    for copy in locals_:
        copy.start()

    barrier = pltpu.get_barrier_semaphore()
    expected = jnp.int32(2)
    for target in (following, preceding):
        pl.semaphore_signal(barrier, inc=1, device_id=(seg, target, c), device_id_type=MESH_ID)
    for dr, dc in offsets:
        there = present(dr, dc)
        expected = expected + there.astype(jnp.int32)

        @pl.when(there)
        def _():
            pl.semaphore_signal(
                barrier, inc=1, device_id=(seg, r + dr, c + dc), device_id_type=MESH_ID
            )

    if shared:
        expected = expected + 1
        pl.semaphore_signal(barrier, inc=1, device_id=(1 - seg, r, c), device_id_type=MESH_ID)
    pl.semaphore_wait(barrier, expected)

    def exchange(number, source_of, buffer, pad, reach, width):
        arrivals, departures = [], []
        for i, (dr, dc) in enumerate((a, b) for a in (-1, 0, 1) for b in (-1, 0, 1)):
            if (dr, dc) == (0, 0) or (dr and not pad):
                continue
            first, span, landing = {
                -1: (0, pad, pad + height), 0: (0, height, pad), 1: (height - pad, pad, 0)
            }[dr]
            left, extent, side = {
                -1: (0, width[1], width[0] + across),
                0: (0, across, width[0]),
                1: (across - width[1], width[1], width[0] - width[1]),
            }[dc]
            copy = pltpu.make_async_remote_copy(
                src_ref=source_of(first, span, left, extent),
                dst_ref=buffer.at[pl.ds(landing, span), pl.ds(side, extent)],
                send_sem=ex_s.at[number, i],
                recv_sem=ex_r.at[number, i],
                device_id=(seg, r + dr * reach, c + dc),
                device_id_type=MESH_ID,
            )
            there, behind = present(dr * reach, dc), present(-dr * reach, -dc)
            pl.when(there)(copy.start)
            departures.append((there, copy))
            arrivals.append((behind, copy))

        def arrive():
            for behind, copy in arrivals:
                pl.when(behind)(copy.wait_recv)

        def depart():
            for there, copy in departures:
                pl.when(there)(copy.wait_send)

        return arrive, depart

    def block_of(buffer, pad, margin):
        return lambda first, span, left, extent: buffer.at[
            pl.ds(pad + first, span), pl.ds(margin + left, extent)
        ]

    departs = []
    frame_arrivals = []
    for t in range(steps):
        arrive, depart = exchange(
            t,
            lambda first, span, left, extent, t=t: frames.at[
                seg, t, pl.ds(first, span), pl.ds(left, extent)
            ],
            fp.at[t], 1, 1, (MARGIN, MARGIN),
        )
        frame_arrivals.append(arrive)
        departs.append(depart)

    parts = (2 * seg, 1, 2 * (1 - seg)) if shared else (0, 1, 2)
    carried = range(2) if shared else range(3)

    def slot(a, part, k):
        span = gathered[a].shape[1] // 3
        source = rows_at((place - sign * k + n) % n)
        return gathered[a].at[source, pl.ds(parts[part] * span, span)]

    def ring_copy(a, part, k, sent=True):
        span = gathered[a].shape[1] // 3
        place_of = slot(a, part, k if sent else k + 1)
        start = (9 - 3 * span) // 2 + parts[part] * span
        return pltpu.make_async_remote_copy(
            src_ref=stored[a].at[pl.ds(start, span)] if sent and k == 0 else place_of,
            dst_ref=place_of,
            send_sem=ring_s.at[a, part, k],
            recv_sem=ring_r.at[a, part, k],
            device_id=ahead_id,
            device_id_type=MESH_ID,
        )

    def across_copy(a, k, sent=True):
        piece = slot(a, 0 if sent else 2, k)
        return pltpu.make_async_remote_copy(
            src_ref=piece, dst_ref=piece, send_sem=across_s.at[a, k], recv_sem=across_r.at[a, k],
            device_id=(1 - seg, r, c), device_id_type=MESH_ID,
        )

    def pair_copy(a, part, k, direction):
        piece = slot(a, part, direction * k)
        return pltpu.make_async_remote_copy(
            src_ref=piece, dst_ref=piece, send_sem=pair_s.at[a, part, k],
            recv_sem=pair_r.at[a, part, k], device_id=partner_id, device_id_type=MESH_ID,
        )

    def longer(a):
        return even_core if a == 0 else odd_core

    def guarded(condition, act):
        if condition is None:
            act()
        else:
            pl.when(condition)(act)

    def ring_send(a, part, k):
        guarded(longer(a) if k == half - 1 else None, ring_copy(a, part, k).start)

    def own_send(a):
        for part in carried:
            ring_send(a, part, 0)

    def ring_step(a, k):
        def act():
            for part in carried:
                ring_copy(a, part, k - 1, False).wait_recv()
                if k < half:
                    ring_send(a, part, k)
                if shared and part == 0:
                    across_copy(a, k).start()
                pair_copy(a, part, k, 1).start()

        guarded(longer(a) if k == half else None, act)

    def across_step(a, k):
        def act():
            across_copy(a, k, False).wait_recv()
            pair_copy(a, 2, k, 1).start()

        if shared:
            guarded(longer(a) if k == half else None, act)

    def pair_waits(a):
        shorter = odd_core if a == 0 else even_core
        for k in range(1, half + 1):
            for part in range(3):
                guarded(
                    shorter if k == half else None, pair_copy(a, part, k, -1).wait_recv
                )

    context_steps = list(range(1, half + 1))
    quarter = max(1, half // 4)

    def context_ring(count):
        for _ in range(min(count, len(context_steps))):
            k = context_steps.pop(0)
            for a in (1, 2, 3):
                ring_step(a, k)
            if k > 1:
                for a in (1, 2, 3):
                    across_step(a, k - 1)

    own_send(0)
    for k in range(1, half + 1):
        ring_step(0, k)
        if k > 1:
            across_step(0, k - 1)
        if k <= 3:
            own_send(k)
    for k in range(half + 1, 4):
        own_send(k)
    context_ring(quarter)
    across_step(0, half)

    for copy in locals_:
        copy.wait()
    for arrive in frame_arrivals:
        arrive()
    pair_waits(0)

    bias = cell_b[...].reshape(1, -1)
    per = wc.shape[2]
    frame_sources = channels // per

    def tap_columns(buffer):
        taps = []
        for row in range(height + 2):
            wide = buffer[row].astype(jnp.float32)
            length = wide.shape[0]
            taps.append(
                [
                    pltpu.roll(wide, 1, 0)[MARGIN : MARGIN + across].astype(jnp.bfloat16),
                    buffer[row, MARGIN : MARGIN + across],
                    pltpu.roll(wide, length - 1, 0)[MARGIN : MARGIN + across].astype(
                        jnp.bfloat16
                    ),
                ]
            )
        return taps

    def gate_part(buffer, sources):
        taps = tap_columns(buffer)
        left = jnp.concatenate(
            [
                jnp.concatenate([taps[row + a][b] for row in range(height)], axis=0)
                for a in range(3)
                for b in range(3)
            ],
            axis=1,
        )
        right = jnp.concatenate([wc[s, t] for t in range(9) for s in sources], axis=0)
        return jnp.dot(left, right, preferred_element_type=jnp.float32)

    def update(gates, memory):
        inflow = jax.nn.sigmoid(gates[:, :state])
        forget = jax.nn.sigmoid(gates[:, state : 2 * state])
        output = jax.nn.sigmoid(gates[:, 2 * state : 3 * state])
        fresh = inflow * jnp.tanh(gates[:, 3 * state :])
        memory = fresh if memory is None else forget * memory + fresh
        return (output * jnp.tanh(memory)).astype(jnp.bfloat16), memory

    seen, unseen = range(frame_sources), range(frame_sources, n)
    hidden, memory = update(gate_part(fp.at[0], seen) + bias, None)
    for t in range(1, steps):
        view = hp.at[t - 1]
        for row in range(height):
            view[1 + row, MARGIN : MARGIN + across] = hidden[row * across : (row + 1) * across]
        arrive, depart = exchange(
            steps + t - 1, block_of(view, 1, MARGIN), view, 1, 1, (MARGIN, MARGIN)
        )
        departs.append(depart)
        context_ring(quarter)
        gates = gate_part(fp.at[t], seen) + bias
        context_ring(quarter)
        arrive()
        hidden, memory = update(gates + gate_part(view, unseen), memory)

    feature = hidden
    layers = ((f1, w1, first_b), (f2, w2, second_b), (f3, w3, third_b))
    for i, (buffer, weight, offset) in enumerate(layers):
        spacing, pad = DILATIONS[i], row_pads[i]
        for row in range(height):
            buffer[pad + row, spacing : spacing + across] = feature[
                row * across : (row + 1) * across
            ]
        arrive, depart = exchange(
            2 * steps - 1 + i, block_of(buffer, pad, spacing), buffer, pad,
            spacing // height, (spacing, spacing),
        )
        departs.append(depart)
        if i == 0:
            context_ring(len(context_steps))
            for a in (1, 2, 3):
                across_step(a, half)
        pair_waits(i + 1)
        arrive()
        total = None
        taps = weight.shape[1]
        for t in range(taps):
            a, b = t // 3, t % 3
            left = buffer[a * pad : a * pad + height, b * spacing : b * spacing + across]
            left = left.reshape(height * across, left.shape[-1])
            right = jnp.concatenate([weight[s, t] for s in range(n)], axis=0)
            product = jnp.dot(left, right, preferred_element_type=jnp.float32)
            total = product if total is None else total + product
        result = jnp.maximum(total + offset[...].reshape(1, -1), 0.0)
        if i < 2:
            feature = result.astype(jnp.bfloat16)
    context = (feature.astype(jnp.float32) + result).astype(jnp.bfloat16)
    out[0] = context.reshape(out.shape[1:])

    for depart in departs:
        depart()
    for a in range(4):
        for k in range(half):
            for part in carried:
                guarded(
                    longer(a) if k == half - 1 else None, ring_copy(a, part, k).wait_send
                )
        for k in range(1, half + 1):
            for part in range(3):
                guarded(longer(a) if k == half else None, pair_copy(a, part, k, 1).wait_send)
            if shared:
                guarded(longer(a) if k == half else None, across_copy(a, k).wait_send)


def per_device(n, cols, shared, *args):
    import functools

    frames, cell_w, cell_b, first_w, first_b, second_w, second_b, third_w, third_b = args
    micro, steps, height, across, channels = frames.shape
    state, width = cell_b.shape[0] // 4, first_b.shape[0]
    row_pads = tuple(height if s // height < n else 0 for s in DILATIONS)

    def slots(weight, pad):
        return pltpu.VMEM((n, 9 if pad else 3) + weight.shape[1:], weight.dtype)

    def field(spacing, pad, depth):
        return pltpu.VMEM((height + 2 * pad, across + 2 * spacing, depth), jnp.bfloat16)

    half = n // 2
    exchanges = 2 * steps - 1 + 3
    dma = pltpu.SemaphoreType.DMA
    anywhere, vmem = pl.BlockSpec(memory_space=pl.ANY), pl.BlockSpec(memory_space=pltpu.VMEM)
    return pl.pallas_call(
        functools.partial(encoder_kernel, n=n, cols=cols, shared=shared, row_pads=row_pads),
        out_shape=jax.ShapeDtypeStruct((1, height, across, width), jnp.bfloat16),
        in_specs=[anywhere, anywhere, vmem, anywhere, vmem, anywhere, vmem, anywhere, vmem],
        out_specs=vmem,
        scratch_shapes=[
            slots(cell_w, 1),
            slots(first_w, row_pads[0]),
            slots(second_w, row_pads[1]),
            slots(third_w, row_pads[2]),
            pltpu.VMEM((steps, height + 2, across + 2 * MARGIN, channels), jnp.bfloat16),
            pltpu.VMEM((steps - 1, height + 2, across + 2 * MARGIN, state), jnp.bfloat16),
            field(DILATIONS[0], row_pads[0], state),
            field(DILATIONS[1], row_pads[1], width),
            field(DILATIONS[2], row_pads[2], width),
            dma((steps + 4,)),
            dma((4, 3, half)),
            dma((4, 3, half)),
            dma((4, half + 1)),
            dma((4, half + 1)),
            dma((4, 3, half + 1)),
            dma((4, 3, half + 1)),
            dma((exchanges, 9)),
            dma((exchanges, 9)),
        ],
        compiler_params=pltpu.CompilerParams(collective_id=0, has_side_effects=True),
    )(
        frames, cell_w, cell_b, first_w, first_b, second_w, second_b,
        third_w, third_b,
    )


def solution(mesh):
    import functools

    kernels = P(None, "rows", None)
    placed = (
        P(None, None, "rows", "cols", None),
        kernels, P(), kernels, P(), kernels, P(), kernels, P(),
    )
    return jax.shard_map(
        functools.partial(per_device, mesh.shape["rows"], mesh.shape["cols"], mesh.shape["segment"] == 2),
        mesh=mesh,
        in_specs=placed,
        out_specs=P("segment", "rows", "cols", None),
        check_vma=False,
    )
```

```python
import jax
import jax.numpy as jnp
from jax import lax
from jax.experimental import pallas as pl
from jax.experimental.pallas import tpu as pltpu
from jax.sharding import PartitionSpec as P

DILATIONS = (16, 32, 64)
MESH_ID = pl.DeviceIdType.MESH
MARGIN = 16


def encoder_kernel(
    frames, cell_w, cell_b, first_w, first_b, second_w, second_b, third_w, third_b,
    out, wc, w1, w2, w3, fp, hp, f1, f2, f3,
    local_sem, ring_s, ring_r, across_s, across_r, pair_s, pair_r, ex_s, ex_r, *, n, cols, shared, row_pads,
):
    seg, r, c = lax.axis_index("segment"), lax.axis_index("rows"), lax.axis_index("cols")
    steps, height, across, channels = frames.shape[1:]
    state = cell_b.shape[-1] // 4
    half = n // 2
    odd = lax.rem(c, 2)
    even_core, odd_core = odd == 0, odd == 1
    sign = 1 - 2 * odd
    parity, pair = lax.rem(r, 2), lax.div(r, 2)
    place = pair + parity * (n - 1 - 2 * pair)

    def rows_at(position):
        upper = lax.div(position, half)
        return 2 * position + upper * (2 * n - 1 - 4 * position)

    behind_rows = [r] + [rows_at(lax.rem(place - sign * k + n, n)) for k in range(1, half + 1)]
    ahead_rows = [r] + [rows_at(lax.rem(place + sign * k + n, n)) for k in range(1, half + 1)]
    following, preceding = ahead_rows[1], behind_rows[1]
    partner = c + 1 - 2 * odd
    ahead_id, partner_id = (seg, following, c), (seg, r, partner)

    reaches = sorted({1} | {s // height for s, pad in zip(DILATIONS, row_pads) if pad})
    offsets = [(0, -1), (0, 1)] + [
        (d * reach, dc) for reach in reaches for d in (-1, 1) for dc in (-1, 0, 1)
    ]

    def present(dr, dc):
        row, col = r + dr, c + dc
        return jnp.logical_and(
            jnp.logical_and(row >= 0, row < n), jnp.logical_and(col >= 0, col < cols)
        )

    inside = {offset: present(*offset) for offset in offsets}

    locals_ = []
    for t in range(steps):
        locals_.append(
            pltpu.make_async_copy(
                frames.at[seg, t],
                fp.at[t, pl.ds(1, height), pl.ds(MARGIN, across)],
                local_sem.at[t],
            )
        )
    stored = (cell_w, first_w, second_w, third_w)
    gathered = (wc, w1, w2, w3)
    own = []
    for ref, whole in zip(stored, gathered):
        taps = whole.shape[1]
        own.append(ref.at[pl.ds((9 - taps) // 2, taps)])
    for a in range(4):
        locals_.append(
            pltpu.make_async_copy(own[a], gathered[a].at[r], local_sem.at[steps + a])
        )
    for t in range(steps):
        fp[t] = jnp.zeros(fp.shape[1:], fp.dtype)
    for t in range(hp.shape[0]):
        hp[t] = jnp.zeros(hp.shape[1:], hp.dtype)
    for buffer in (f1, f2, f3):
        buffer[...] = jnp.zeros(buffer.shape, buffer.dtype)
    for copy in locals_:
        copy.start()

    barrier = pltpu.get_barrier_semaphore()
    expected = jnp.int32(2)
    for target in (following, preceding):
        pl.semaphore_signal(barrier, inc=1, device_id=(seg, target, c), device_id_type=MESH_ID)
    for dr, dc in offsets:
        there = inside[dr, dc]
        expected = expected + there.astype(jnp.int32)

        @pl.when(there)
        def _():
            pl.semaphore_signal(
                barrier, inc=1, device_id=(seg, r + dr, c + dc), device_id_type=MESH_ID
            )

    if shared:
        expected = expected + 1
        pl.semaphore_signal(barrier, inc=1, device_id=(1 - seg, r, c), device_id_type=MESH_ID)
    pl.semaphore_wait(barrier, expected)

    def exchange(number, source_of, buffer, pad, reach, width):
        arrivals, departures = [], []
        for i, (dr, dc) in enumerate((a, b) for a in (-1, 0, 1) for b in (-1, 0, 1)):
            if (dr, dc) == (0, 0) or (dr and not pad):
                continue
            first, span, landing = {
                -1: (0, pad, pad + height), 0: (0, height, pad), 1: (height - pad, pad, 0)
            }[dr]
            left, extent, side = {
                -1: (0, width[1], width[0] + across),
                0: (0, across, width[0]),
                1: (across - width[1], width[1], width[0] - width[1]),
            }[dc]
            copy = pltpu.make_async_remote_copy(
                src_ref=source_of(first, span, left, extent),
                dst_ref=buffer.at[pl.ds(landing, span), pl.ds(side, extent)],
                send_sem=ex_s.at[number, i],
                recv_sem=ex_r.at[number, i],
                device_id=(seg, r + dr * reach, c + dc),
                device_id_type=MESH_ID,
            )
            there, behind = inside[dr * reach, dc], inside[-dr * reach, -dc]
            pl.when(there)(copy.start)
            departures.append((there, copy))
            arrivals.append((behind, copy))

        def arrive():
            for behind, copy in arrivals:
                pl.when(behind)(copy.wait_recv)

        def depart():
            for there, copy in departures:
                pl.when(there)(copy.wait_send)

        return arrive, depart

    def block_of(buffer, pad, margin):
        return lambda first, span, left, extent: buffer.at[
            pl.ds(pad + first, span), pl.ds(margin + left, extent)
        ]

    departs = []
    frame_arrivals = []
    for t in range(steps):
        arrive, depart = exchange(
            t,
            lambda first, span, left, extent, t=t: frames.at[
                seg, t, pl.ds(first, span), pl.ds(left, extent)
            ],
            fp.at[t], 1, 1, (MARGIN, MARGIN),
        )
        frame_arrivals.append(arrive)
        departs.append(depart)

    parts = (2 * seg, 1, 2 * (1 - seg)) if shared else (0, 1, 2)
    carried = range(2) if shared else range(3)

    def slot(a, part, k):
        span = gathered[a].shape[1] // 3
        source = behind_rows[k] if k >= 0 else ahead_rows[-k]
        return gathered[a].at[source, pl.ds(parts[part] * span, span)]

    def ring_copy(a, part, k, sent=True):
        span = gathered[a].shape[1] // 3
        place_of = slot(a, part, k if sent else k + 1)
        start = (9 - 3 * span) // 2 + parts[part] * span
        return pltpu.make_async_remote_copy(
            src_ref=stored[a].at[pl.ds(start, span)] if sent and k == 0 else place_of,
            dst_ref=place_of,
            send_sem=ring_s.at[a, part, k],
            recv_sem=ring_r.at[a, part, k],
            device_id=ahead_id,
            device_id_type=MESH_ID,
        )

    def across_copy(a, k, sent=True):
        piece = slot(a, 0 if sent else 2, k)
        return pltpu.make_async_remote_copy(
            src_ref=piece, dst_ref=piece, send_sem=across_s.at[a, k], recv_sem=across_r.at[a, k],
            device_id=(1 - seg, r, c), device_id_type=MESH_ID,
        )

    def pair_copy(a, part, k, direction):
        piece = slot(a, part, direction * k)
        return pltpu.make_async_remote_copy(
            src_ref=piece, dst_ref=piece, send_sem=pair_s.at[a, part, k],
            recv_sem=pair_r.at[a, part, k], device_id=partner_id, device_id_type=MESH_ID,
        )

    def longer(a):
        return even_core if a == 0 else odd_core

    def guarded(condition, act):
        if condition is None:
            act()
        else:
            pl.when(condition)(act)

    def ring_send(a, part, k):
        guarded(longer(a) if k == half - 1 else None, ring_copy(a, part, k).start)

    def own_send(a):
        for part in carried:
            ring_send(a, part, 0)

    def ring_step(a, k):
        def act():
            for part in carried:
                ring_copy(a, part, k - 1, False).wait_recv()
                if k < half:
                    ring_send(a, part, k)
                if shared and part == 0:
                    across_copy(a, k).start()
                pair_copy(a, part, k, 1).start()

        guarded(longer(a) if k == half else None, act)

    def across_step(a, k):
        def act():
            across_copy(a, k, False).wait_recv()
            pair_copy(a, 2, k, 1).start()

        if shared:
            guarded(longer(a) if k == half else None, act)

    def pair_waits(a):
        shorter = odd_core if a == 0 else even_core
        for k in range(1, half + 1):
            for part in range(3):
                guarded(
                    shorter if k == half else None, pair_copy(a, part, k, -1).wait_recv
                )

    context_steps = list(range(1, half + 1))
    quarter = max(1, half // 4)

    def context_ring(count):
        for _ in range(min(count, len(context_steps))):
            k = context_steps.pop(0)
            for a in (1, 2, 3):
                ring_step(a, k)
            if k > 1:
                for a in (1, 2, 3):
                    across_step(a, k - 1)

    own_send(0)
    for k in range(1, half + 1):
        ring_step(0, k)
        if k > 1:
            across_step(0, k - 1)
        if k == 1:
            for a in (1, 2, 3):
                own_send(a)
        else:
            context_ring(1)
    context_ring(quarter)
    across_step(0, half)

    for copy in locals_:
        copy.wait()
    for arrive in frame_arrivals:
        arrive()
    pair_waits(0)

    bias = cell_b[...].reshape(1, -1)
    per = wc.shape[2]
    frame_sources = channels // per

    def tap_columns(buffer):
        taps = []
        for row in range(height + 2):
            wide = buffer[row].astype(jnp.float32)
            length = wide.shape[0]
            taps.append(
                [
                    pltpu.roll(wide, 1, 0)[MARGIN : MARGIN + across].astype(jnp.bfloat16),
                    buffer[row, MARGIN : MARGIN + across],
                    pltpu.roll(wide, length - 1, 0)[MARGIN : MARGIN + across].astype(
                        jnp.bfloat16
                    ),
                ]
            )
        return taps

    def gate_part(buffer, sources):
        taps = tap_columns(buffer)
        left = jnp.concatenate(
            [
                jnp.concatenate([taps[row + a][b] for row in range(height)], axis=0)
                for a in range(3)
                for b in range(3)
            ],
            axis=1,
        )
        right = jnp.concatenate([wc[s, t] for t in range(9) for s in sources], axis=0)
        return jnp.dot(left, right, preferred_element_type=jnp.float32)

    def update(gates, memory):
        inflow = jax.nn.sigmoid(gates[:, :state])
        forget = jax.nn.sigmoid(gates[:, state : 2 * state])
        output = jax.nn.sigmoid(gates[:, 2 * state : 3 * state])
        fresh = inflow * jnp.tanh(gates[:, 3 * state :])
        memory = fresh if memory is None else forget * memory + fresh
        return (output * jnp.tanh(memory)).astype(jnp.bfloat16), memory

    seen, unseen = range(frame_sources), range(frame_sources, n)
    hidden, memory = update(gate_part(fp.at[0], seen) + bias, None)
    for t in range(1, steps):
        view = hp.at[t - 1]
        for row in range(height):
            view[1 + row, MARGIN : MARGIN + across] = hidden[row * across : (row + 1) * across]
        arrive, depart = exchange(
            steps + t - 1, block_of(view, 1, MARGIN), view, 1, 1, (MARGIN, MARGIN)
        )
        departs.append(depart)
        context_ring(quarter)
        gates = gate_part(fp.at[t], seen) + bias
        context_ring(quarter)
        arrive()
        hidden, memory = update(gates + gate_part(view, unseen), memory)

    feature = hidden
    layers = ((f1, w1, first_b), (f2, w2, second_b), (f3, w3, third_b))
    for i, (buffer, weight, offset) in enumerate(layers):
        spacing, pad = DILATIONS[i], row_pads[i]
        for row in range(height):
            buffer[pad + row, spacing : spacing + across] = feature[
                row * across : (row + 1) * across
            ]
        arrive, depart = exchange(
            2 * steps - 1 + i, block_of(buffer, pad, spacing), buffer, pad,
            spacing // height, (spacing, spacing),
        )
        departs.append(depart)
        if i == 0:
            context_ring(len(context_steps))
            for a in (1, 2, 3):
                across_step(a, half)
        pair_waits(i + 1)
        arrive()
        total = None
        taps = weight.shape[1]
        for t in range(taps):
            a, b = t // 3, t % 3
            left = buffer[a * pad : a * pad + height, b * spacing : b * spacing + across]
            left = left.reshape(height * across, left.shape[-1])
            right = jnp.concatenate([weight[s, t] for s in range(n)], axis=0)
            product = jnp.dot(left, right, preferred_element_type=jnp.float32)
            total = product if total is None else total + product
        result = jnp.maximum(total + offset[...].reshape(1, -1), 0.0)
        if i < 2:
            feature = result.astype(jnp.bfloat16)
    context = (feature.astype(jnp.float32) + result).astype(jnp.bfloat16)
    out[0] = context.reshape(out.shape[1:])

    for depart in departs:
        depart()
    for a in range(4):
        for k in range(half):
            for part in carried:
                guarded(
                    longer(a) if k == half - 1 else None, ring_copy(a, part, k).wait_send
                )
        for k in range(1, half + 1):
            for part in range(3):
                guarded(longer(a) if k == half else None, pair_copy(a, part, k, 1).wait_send)
            if shared:
                guarded(longer(a) if k == half else None, across_copy(a, k).wait_send)


def per_device(n, cols, shared, *args):
    import functools

    frames, cell_w, cell_b, first_w, first_b, second_w, second_b, third_w, third_b = args
    micro, steps, height, across, channels = frames.shape
    state, width = cell_b.shape[0] // 4, first_b.shape[0]
    row_pads = tuple(height if s // height < n else 0 for s in DILATIONS)

    def slots(weight, pad):
        return pltpu.VMEM((n, 9 if pad else 3) + weight.shape[1:], weight.dtype)

    def field(spacing, pad, depth):
        return pltpu.VMEM((height + 2 * pad, across + 2 * spacing, depth), jnp.bfloat16)

    half = n // 2
    exchanges = 2 * steps - 1 + 3
    dma = pltpu.SemaphoreType.DMA
    anywhere, vmem = pl.BlockSpec(memory_space=pl.ANY), pl.BlockSpec(memory_space=pltpu.VMEM)
    return pl.pallas_call(
        functools.partial(encoder_kernel, n=n, cols=cols, shared=shared, row_pads=row_pads),
        out_shape=jax.ShapeDtypeStruct((1, height, across, width), jnp.bfloat16),
        in_specs=[anywhere, anywhere, vmem, anywhere, vmem, anywhere, vmem, anywhere, vmem],
        out_specs=vmem,
        scratch_shapes=[
            slots(cell_w, 1),
            slots(first_w, row_pads[0]),
            slots(second_w, row_pads[1]),
            slots(third_w, row_pads[2]),
            pltpu.VMEM((steps, height + 2, across + 2 * MARGIN, channels), jnp.bfloat16),
            pltpu.VMEM((steps - 1, height + 2, across + 2 * MARGIN, state), jnp.bfloat16),
            field(DILATIONS[0], row_pads[0], state),
            field(DILATIONS[1], row_pads[1], width),
            field(DILATIONS[2], row_pads[2], width),
            dma((steps + 4,)),
            dma((4, 3, half)),
            dma((4, 3, half)),
            dma((4, half + 1)),
            dma((4, half + 1)),
            dma((4, 3, half + 1)),
            dma((4, 3, half + 1)),
            dma((exchanges, 9)),
            dma((exchanges, 9)),
        ],
        compiler_params=pltpu.CompilerParams(collective_id=0, has_side_effects=True),
    )(
        frames, cell_w, cell_b, first_w, first_b, second_w, second_b,
        third_w, third_b,
    )


def solution(mesh):
    import functools

    kernels = P(None, "rows", None)
    placed = (
        P(None, None, "rows", "cols", None),
        kernels, P(), kernels, P(), kernels, P(), kernels, P(),
    )
    return jax.shard_map(
        functools.partial(per_device, mesh.shape["rows"], mesh.shape["cols"], mesh.shape["segment"] == 2),
        mesh=mesh,
        in_specs=placed,
        out_specs=P("segment", "rows", "cols", None),
        check_vma=False,
    )
```
